32 devices in a mesh: replica: 8 (over y, x, core), tensor: 4 (over z).
Axes of the slice: x: 2, y: 2, z: 4, core: 2. Of those that a mesh axis runs over, the one named last changes fastest.
Arguments:
- weight: bfloat16 [8, 4096, 2048], P('replica', None, 'tensor'), may hold values from -0.09375 to 0.09375
- momentum: bfloat16 [8, 4096, 2048], P('replica', None, 'tensor'), may hold values from -24 to 24
- inputs: bfloat16 [2, 4096, 4096], P(None, ('replica', 'tensor')), may hold values from -6 to 6
- out_grads: bfloat16 [2, 4096, 2048], P(None, 'replica', 'tensor'), may hold values from -6 to 6
Outputs:
- new_weight: bfloat16 [8, 4096, 2048], P('replica', None, 'tensor')
- new_momentum: bfloat16 [8, 4096, 2048], P('replica', None, 'tensor')
- input_grad: bfloat16 [2, 4096, 4096], P(None, ('replica', 'tensor'))
The draws below stay inside these ranges and needn't reach their ends.
All inputs are finite; a program needn't handle non-finite values.
Results may differ from the reference program's by a relative error of at most 0.014.
Values may be sent and summed in bfloat16 or wider, within the bound.
No kernel may reach another device: no remote copies, remote signals or barrier semaphores. Data moves between devices by JAX's collectives and lax.ppermute only.
A program may use at most 128 MiB of HBM per device.

```python
import jax
import jax.numpy as jnp
from jax import lax

D = 4096
DOUT = 2048
ROWS = 512
STEPS = 2
REPLICAS = 8
TOTAL_ROWS = 4096
N_TENSOR = 4


def levels(stream_key, dims, split, least, top_value):
    level = 1.0
    for position, blocks in split:
        heights = jax.random.uniform(jax.random.fold_in(jax.random.fold_in(stream_key, 6), position), (blocks,), jnp.float32, least / len(split), top_value / len(split))
        level = level * jnp.repeat(jnp.exp(heights), dims[position] // blocks).reshape((-1,) + (1,) * (len(dims) - 1 - position))
    return level


def gaussian(rng, extent, scale, most, shards=(), kind=jnp.bfloat16):
    result = jax.random.normal(rng, extent, jnp.float32) * scale
    if len(shards) > 0:
        result = levels(rng, extent, shards, -0.22, 0.18) * result
    return jnp.clip(result, min=-most, max=most).astype(kind)


def setup_inputs(seed: int = 0) -> dict:
    seeds = jax.random.split(jax.random.key(seed), 5)
    return {
        "weight": gaussian(seeds[0], (REPLICAS, D, DOUT), D ** -0.5, 0.09375, ((0, 8), (2, 4))),
        "momentum": gaussian(seeds[1], (REPLICAS, D, DOUT), 4.0, 24.0, ((0, 8), (2, 4))),
        "inputs": gaussian(seeds[2], (STEPS, TOTAL_ROWS, D), 1.0, 6.0, ((1, 32),)),
        "out_grads": gaussian(seeds[3], (STEPS, TOTAL_ROWS, DOUT), 1.0, 6.0, ((1, 8), (2, 4))),
    }


learn_rate = 0.001
mom_decay = 0.9


def silu_slope(pre):
    sigma = jax.nn.sigmoid(pre)
    return sigma * (1.0 + pre * (1.0 - sigma))


def reference(weight, momentum, inputs, out_grads):
    replicas = weight.shape[0]
    indices = jnp.arange(replicas, dtype=jnp.int32)
    blocks = DOUT // N_TENSOR
    weight_now = weight
    moment_now = momentum
    grads_out = []
    for step in range(STEPS):
        rows_in = inputs[step].reshape(replicas, ROWS, D).astype(jnp.float32)
        pre = jnp.einsum('rnd,rdk->rnk', rows_in, weight_now.astype(jnp.float32))
        upstream = out_grads[step].reshape(replicas, ROWS, DOUT).astype(jnp.float32)
        slope_grad = (upstream * silu_slope(pre)).astype(jnp.bfloat16)
        grad_w = jnp.einsum('rnd,rnk->rdk', rows_in, slope_grad.astype(jnp.float32))
        partial_value = jnp.einsum('rntc,rdtc->rtnd',
                             slope_grad.reshape(replicas, ROWS, N_TENSOR, blocks).astype(jnp.float32),
                             weight_now.reshape(replicas, D, N_TENSOR, blocks).astype(jnp.float32))
        partial_value = lax.optimization_barrier(partial_value.astype(jnp.bfloat16)).astype(jnp.float32)
        grads_out.append(jnp.sum(partial_value, axis=1).astype(jnp.bfloat16).reshape(replicas * ROWS, D))
        moment_new = (mom_decay * moment_now.astype(jnp.float32) + grad_w).astype(jnp.bfloat16)
        stepped = (weight_now.astype(jnp.float32) - learn_rate * moment_new.astype(jnp.float32)).astype(jnp.bfloat16)
        partner = jnp.bitwise_xor(indices, jnp.int32(1 << step))
        weight_now = ((stepped.astype(jnp.float32) + stepped[partner].astype(jnp.float32)) * 0.5).astype(jnp.bfloat16)
        moment_now = ((moment_new.astype(jnp.float32) + moment_new[partner].astype(jnp.float32)) * 0.5).astype(jnp.bfloat16)
    return weight_now, moment_now, jnp.stack(grads_out)
```

```python
import functools

import jax
import jax.numpy as jnp
from jax import lax
from jax.experimental import pallas as pl
from jax.experimental.pallas import tpu as pltpu
from jax.sharding import PartitionSpec as P

learn_rate = 0.001
mom_decay = 0.9
n_chunks = 4


def xor_route(count, mask):
    return [(r, r ^ mask) for r in range(count) if r ^ mask < count]


def silu_slope(pre):
    sigma = jax.nn.sigmoid(pre)
    return sigma * (1.0 + pre * (1.0 - sigma))


def f32(a):
    return a.astype(jnp.float32)


def grad_body(decay, *refs):
    n = (len(refs) - 2) // 2
    x = jnp.concatenate([r[...] for r in refs[:n]], axis=0)
    s = jnp.concatenate([r[...] for r in refs[n : 2 * n]], axis=0)
    grad = lax.dot_general(x, s, (((0,), (0,)), ((), ())), preferred_element_type=jnp.float32)
    refs[-1][...] = (decay * f32(refs[-2][...]) + grad).astype(jnp.bfloat16)


def moment_step(blocks, slopes, moment, chunk, chunks):
    rows, width = blocks[0].shape
    cols = slopes[0].shape[1]
    size = width // chunks
    tile = min(512, size)
    steps = size // tile
    first = chunk * steps
    return pl.pallas_call(
        functools.partial(grad_body, mom_decay),
        grid=(steps,),
        in_specs=[pl.BlockSpec((rows, tile), lambda i: (0, first + i))] * len(blocks)
        + [pl.BlockSpec((rows, cols), lambda i: (0, 0))] * len(slopes)
        + [pl.BlockSpec((tile, cols), lambda i: (first + i, 0))],
        out_specs=pl.BlockSpec((tile, cols), lambda i: (i, 0)),
        out_shape=jax.ShapeDtypeStruct((size, cols), jnp.bfloat16),
        name="moment_step",
    )(*blocks, *slopes, moment)


def final_body(m_ref, mp_ref, wa_ref, wb_ref, *refs):
    w_out, m_out = refs[-2:]
    mean = 0.5 * (f32(m_ref[...]) + f32(mp_ref[...]))
    m_out[...] = mean.astype(jnp.bfloat16)
    w_out[...] = (0.5 * (f32(wa_ref[...]) + f32(wb_ref[...])) - learn_rate * mean).astype(jnp.bfloat16)


def final_step(m, mp, wa, wb, chunk, outs, shape):
    size, cols = m.shape
    tile = min(512, size)
    steps = size // tile
    first = chunk * steps
    part = pl.BlockSpec((tile, cols), lambda i: (i, 0))
    whole = pl.BlockSpec((tile, cols), lambda i: (first + i, 0))
    return pl.pallas_call(
        final_body,
        grid=(steps,),
        in_specs=[part, part, whole, whole] + [pl.BlockSpec(memory_space=pl.ANY)] * len(outs),
        out_specs=[whole, whole],
        out_shape=[jax.ShapeDtypeStruct(shape, jnp.bfloat16)] * 2,
        input_output_aliases={4 + i: i for i in range(len(outs))},
        name="final_step",
    )(m, mp, wa, wb, *outs)


def up(block, k):
    n = lax.axis_size("tensor")
    return lax.ppermute(block, "tensor", [(i, i + 1) for i in range(k, n - 1)])


def down(block, k):
    n = lax.axis_size("tensor")
    return lax.ppermute(block, "tensor", [(i, i - 1) for i in range(1, n - k)])


def gather(block):
    n = lax.axis_size("tensor")
    t = lax.axis_index("tensor")
    ups, downs = [block], [block]
    for k in range(n - 1):
        ups.append(up(ups[-1], k))
        downs.append(down(downs[-1], k))
    slots = [block] + [jnp.where(t >= k, ups[k], downs[n - k]) for k in range(1, n)]
    late = (ups[max(n - 2, 0)], downs[max(n - 2, 0)])
    return slots, late


def scatter(parts):
    n = len(parts)
    down_sum = up_sum = None
    for d in range(n - 1, 0, -1):
        a = parts[d] if down_sum is None else (f32(parts[d]) + f32(down_sum)).astype(jnp.bfloat16)
        b = parts[n - d] if up_sum is None else (f32(parts[n - d]) + f32(up_sum)).astype(jnp.bfloat16)
        down_sum = lax.ppermute(a, "tensor", [(i, i - 1) for i in range(d, n)])
        up_sum = lax.ppermute(b, "tensor", [(i, i + 1) for i in range(n - d)])
    total = f32(parts[0])
    if n > 1:
        total = total + f32(down_sum) + f32(up_sum)
    return total.astype(jnp.bfloat16)


def slopes_of(slots, grads, weight):
    n = lax.axis_size("tensor")
    t = lax.axis_index("tensor")
    rows = slots[0].shape[0]
    out = []
    for k, block in enumerate(slots):
        pre = jnp.dot(block, weight, preferred_element_type=jnp.float32)
        g = lax.dynamic_slice_in_dim(grads, lax.rem(t - k + n, n) * rows, rows)
        out.append((f32(g) * silu_slope(pre)).astype(jnp.bfloat16))
    return out


def partials_of(slopes, weight):
    return [
        lax.dot_general(s, weight, (((1,), (1,)), ((), ())), preferred_element_type=jnp.float32).astype(jnp.bfloat16)
        for s in slopes
    ]


def local(weight, momentum, inputs, out_grads):
    replicas = lax.axis_size("replica")
    r = lax.axis_index("replica")
    w, m = weight[0], momentum[0]
    steps = inputs.shape[0]
    slots, late = gather(inputs[0])
    grads_out = []
    for step in range(steps):
        last = step == steps - 1
        route = xor_route(replicas, 1 << step)
        if not last:
            following, _, _ = lax.optimization_barrier((inputs[step + 1],) + late)
            next_slots, late = gather(following)
        if step == 0:
            w_other = lax.ppermute(w, "replica", route)
        else:
            half = w.shape[0] // 2
            odd = r & 1
            mine = lax.dynamic_slice_in_dim(w, odd * half, half)
            got = lax.ppermute(mine, "replica", route)
            twin = lax.ppermute(got, "replica", xor_route(replicas, 1))
            w_other = jnp.concatenate([jnp.where(odd == 0, got, twin), jnp.where(odd == 0, twin, got)])
        slopes = slopes_of(slots, out_grads[step], w)
        chunks = n_chunks if last else 1
        moments = [moment_step(slots, slopes, m, c, chunks) for c in range(chunks)]
        others = [lax.ppermute(a, "replica", route) for a in moments]
        grads_out.append(scatter(partials_of(slopes, w)))
        if last:
            outs = []
            for c in range(chunks):
                outs = final_step(moments[c], others[c], w, w_other, c, outs, w.shape)
            w, m = outs
        else:
            mean = 0.5 * (f32(moments[0]) + f32(others[0]))
            w = (0.5 * (f32(w) + f32(w_other)) - learn_rate * mean).astype(jnp.bfloat16)
            m = mean.astype(jnp.bfloat16)
            slots = next_slots
    return (w[None], m[None], jnp.stack(grads_out))


def solution(mesh):
    return jax.shard_map(
        local,
        mesh=mesh,
        in_specs=(
            P("replica", None, "tensor"),
            P("replica", None, "tensor"),
            P(None, ("replica", "tensor"), None),
            P(None, "replica", "tensor"),
        ),
        out_specs=(
            P("replica", None, "tensor"),
            P("replica", None, "tensor"),
            P(None, ("replica", "tensor"), None),
        ),
        check_vma=False,
    )
```

```python
import functools

import jax
import jax.numpy as jnp
from jax import lax
from jax.experimental import pallas as pl
from jax.experimental.pallas import tpu as pltpu
from jax.sharding import PartitionSpec as P


learn_rate = 0.001
mom_decay = 0.9
first_chunks = 2
last_chunks = 4
tile = 512


def f32(a):
    return a.astype(jnp.float32)


def silu_slope(pre):
    sigma = jax.nn.sigmoid(pre)
    return sigma * (1.0 + pre * (1.0 - sigma))


def slope_body(group, n, place, *refs):
    count = len(group)
    cands, (w_ref, g_ref, x_ref, s_ref, acc) = refs[: 2 * count], refs[2 * count :]
    t = place[0]
    rows = x_ref.shape[0] // count
    i = pl.program_id(0)
    for j, k in enumerate(group):
        part = pl.ds(j * rows, rows)

        @pl.when(t >= k)
        def _():
            x_ref[part, :] = cands[2 * j][...]

        @pl.when(t < k)
        def _():
            x_ref[part, :] = cands[2 * j + 1][...]

    got = jnp.dot(x_ref[...], w_ref[...], preferred_element_type=jnp.float32)

    @pl.when(i == 0)
    def _():
        acc[...] = got

    @pl.when(i > 0)
    def _():
        acc[...] += got

    @pl.when(i == pl.num_programs(0) - 1)
    def _():
        for j, k in enumerate(group):
            part = pl.ds(j * rows, rows)
            shard = lax.rem(t - k + n, n)
            g = f32(g_ref[pl.ds(pl.multiple_of(shard * rows, rows), rows), :])
            s_ref[part, :] = (g * silu_slope(acc[part, :])).astype(jnp.bfloat16)


def slope_step(group, n, place, pairs, weight, grads):
    rows, width = pairs[0][0].shape
    cols = weight.shape[1]
    count = len(group)
    size = min(4 * tile, width)
    flat = [a for pair in pairs for a in pair]
    return pl.pallas_call(
        functools.partial(slope_body, group, n),
        grid_spec=pltpu.PrefetchScalarGridSpec(
            num_scalar_prefetch=1,
            grid=(width // size,),
            in_specs=[pl.BlockSpec((rows, size), lambda i, p: (0, i))] * len(flat)
            + [pl.BlockSpec((size, cols), lambda i, p: (i, 0)), pl.BlockSpec(grads.shape, lambda i, p: (0, 0))],
            out_specs=[
                pl.BlockSpec((count * rows, size), lambda i, p: (0, i)),
                pl.BlockSpec((count * rows, cols), lambda i, p: (0, 0)),
            ],
            scratch_shapes=[pltpu.VMEM((count * rows, cols), jnp.float32)],
        ),
        out_shape=[
            jax.ShapeDtypeStruct((count * rows, width), jnp.bfloat16),
            jax.ShapeDtypeStruct((count * rows, cols), jnp.bfloat16),
        ],
        name="slope_step",
    )(place, *flat, weight, grads)


def partial_body(s_ref, w_ref, *outs):
    value = lax.dot_general(
        s_ref[...], w_ref[...], (((1,), (1,)), ((), ())), preferred_element_type=jnp.float32
    ).astype(jnp.bfloat16)
    rows = outs[0].shape[0]
    for j, out in enumerate(outs):
        out[...] = value[j * rows : (j + 1) * rows]


def partial_step(slope, weight, count):
    width, cols = weight.shape
    rows = slope.shape[0] // count
    size = min(4 * tile, width)
    return pl.pallas_call(
        partial_body,
        grid=(width // size,),
        in_specs=[pl.BlockSpec(slope.shape, lambda i: (0, 0)), pl.BlockSpec((size, cols), lambda i: (i, 0))],
        out_specs=[pl.BlockSpec((rows, size), lambda i: (0, i))] * count,
        out_shape=[jax.ShapeDtypeStruct((rows, width), jnp.bfloat16)] * count,
        name="partial_step",
    )(slope, weight)


def moment_body(count, *refs):
    x = jnp.concatenate([r[...] for r in refs[:count]], axis=0)
    s = jnp.concatenate([r[...] for r in refs[count : 2 * count]], axis=0)
    grad = lax.dot_general(x, s, (((0,), (0,)), ((), ())), preferred_element_type=jnp.float32)
    refs[-1][...] = (mom_decay * f32(refs[-2][...]) + grad).astype(jnp.bfloat16)


def moment_step(blocks, slopes, moment, chunk, chunks):
    width, cols = moment.shape
    size = min(2 * tile, width // chunks // 2)
    steps = width // chunks // size
    first = chunk * steps
    return pl.pallas_call(
        functools.partial(moment_body, len(blocks)),
        grid=(steps,),
        in_specs=[pl.BlockSpec((b.shape[0], size), lambda i: (0, first + i)) for b in blocks]
        + [pl.BlockSpec(s.shape, lambda i: (0, 0)) for s in slopes]
        + [pl.BlockSpec((size, cols), lambda i: (first + i, 0))],
        out_specs=pl.BlockSpec((size, cols), lambda i: (i, 0)),
        out_shape=jax.ShapeDtypeStruct((width // chunks, cols), jnp.bfloat16),
        name="moment_step",
    )(*blocks, *slopes, moment)


def mean_body(half, place, m_ref, mp_ref, w_ref, wp_ref, *refs):
    w_out, m_out, mine = refs[-3:]
    mean = 0.5 * (f32(m_ref[...]) + f32(mp_ref[...]))
    m_out[...] = mean.astype(jnp.bfloat16)
    new = (0.5 * (f32(w_ref[...]) + f32(wp_ref[...])) - learn_rate * mean).astype(jnp.bfloat16)
    w_out[...] = new
    at = pl.program_id(0) - place[1] * half

    @pl.when((at >= 0) & (at < half))
    def _():
        mine[...] = new


def mean_step(place, m, mp, w, wp, chunk, outs):
    rows, cols = m.shape
    size = min(tile, rows // 2)
    steps = rows // size
    half = steps // 2
    first = chunk * steps
    part = pl.BlockSpec((size, cols), lambda i, p: (i, 0))
    whole = pl.BlockSpec((size, cols), lambda i, p: (first + i, 0))
    return pl.pallas_call(
        functools.partial(mean_body, half),
        grid_spec=pltpu.PrefetchScalarGridSpec(
            num_scalar_prefetch=1,
            grid=(steps,),
            in_specs=[part, part, whole, whole] + [pl.BlockSpec(memory_space=pl.ANY)] * len(outs),
            out_specs=[
                whole,
                whole,
                pl.BlockSpec((size, cols), lambda i, p: (jnp.clip(i - p[1] * half, 0, half - 1), 0)),
            ],
        ),
        out_shape=[jax.ShapeDtypeStruct(w.shape, jnp.bfloat16)] * 2
        + [jax.ShapeDtypeStruct((rows // 2, cols), jnp.bfloat16)],
        input_output_aliases={5 + i: i for i in range(len(outs))},
        name="mean_step",
    )(place, m, mp, w, wp, *outs)


def final_body(part, place, m_ref, mp_ref, wa_ref, got_ref, twin_ref, *refs):
    w_out, m_out = refs[-2:]
    mean = 0.5 * (f32(m_ref[...]) + f32(mp_ref[...]))
    m_out[...] = mean.astype(jnp.bfloat16)

    def store(wb):
        w_out[...] = (0.5 * (f32(wa_ref[...]) + f32(wb)) - learn_rate * mean).astype(jnp.bfloat16)

    @pl.when(place[1] == part)
    def _():
        store(got_ref[...])

    @pl.when(place[1] != part)
    def _():
        store(twin_ref[...])


def final_step(place, m, mp, wa, got, twin, chunk, outs):
    rows, cols = m.shape
    size = min(tile, rows)
    steps = rows // size
    first = chunk * steps
    part = pl.BlockSpec((size, cols), lambda i, p: (i, 0))
    whole = pl.BlockSpec((size, cols), lambda i, p: (first + i, 0))
    return pl.pallas_call(
        functools.partial(final_body, chunk % 2),
        grid_spec=pltpu.PrefetchScalarGridSpec(
            num_scalar_prefetch=1,
            grid=(steps,),
            in_specs=[part, part, whole, part, part] + [pl.BlockSpec(memory_space=pl.ANY)] * len(outs),
            out_specs=[whole, whole],
        ),
        out_shape=[jax.ShapeDtypeStruct(wa.shape, jnp.bfloat16)] * 2,
        input_output_aliases={6 + i: i for i in range(len(outs))},
        name="final_step",
    )(place, m, mp, wa, got, twin, *outs)


def xor_route(count, mask):
    return [(r, r ^ mask) for r in range(count) if r ^ mask < count]


def gather(block):
    n = lax.axis_size("tensor")
    ups, downs = [block], [block]
    for k in range(n - 1):
        ups.append(lax.ppermute(ups[-1], "tensor", [(i, i + 1) for i in range(k, n - 1)]))
        downs.append(lax.ppermute(downs[-1], "tensor", [(i, i - 1) for i in range(1, n - k)]))
    return ups, downs


def scatter(parts):
    n = len(parts)
    down_sum = up_sum = None
    for d in range(n - 1, 0, -1):
        a = parts[d] if down_sum is None else (f32(parts[d]) + f32(down_sum)).astype(jnp.bfloat16)
        b = parts[n - d] if up_sum is None else (f32(parts[n - d]) + f32(up_sum)).astype(jnp.bfloat16)
        up_sum = lax.ppermute(b, "tensor", [(i, i + 1) for i in range(n - d)])
        down_sum = lax.ppermute(a, "tensor", [(i, i - 1) for i in range(d, n)])
    total = f32(parts[0])
    if n > 1:
        total = total + f32(down_sum) + f32(up_sum)
    return total.astype(jnp.bfloat16)


def groups_of(n):
    late = sorted({1, n - 1})
    early = [k for k in range(n) if k not in late]
    return [g for g in (early, late) if g]


def slopes_of(place, chains, weight, grads):
    ups, downs = chains
    n = len(ups)
    xs, ss = [], []
    for group in groups_of(n):
        pairs = [(ups[k], downs[n - k] if k else downs[0]) for k in group]
        x, s = slope_step(group, n, place, pairs, weight, grads)
        xs.append(x)
        ss.append(s)
    return xs, ss


def partials_of(slopes, weight, n):
    parts = [None] * n
    groups = groups_of(n)
    for j in reversed(range(len(groups))):
        outs = partial_step(slopes[j], weight, len(groups[j]))
        for k, out in zip(groups[j], outs):
            parts[k] = out
    return parts


def local(weight, momentum, inputs, out_grads):
    replicas = lax.axis_size("replica")
    n = lax.axis_size("tensor")
    r = lax.axis_index("replica")
    place = jnp.stack([lax.axis_index("tensor"), r & 1]).astype(jnp.int32)
    w, m = weight[0], momentum[0]
    twins = xor_route(replicas, 1)
    partners = xor_route(replicas, 2)

    chains = gather(inputs[0])
    wp = lax.ppermute(w, "replica", twins)
    late = max(n - 2, 0)
    following, _, _ = lax.optimization_barrier((inputs[1], chains[0][late], chains[1][late]))
    next_chains = gather(following)

    xs, ss = slopes_of(place, chains, w, out_grads[0])
    moments = []
    for c in range(first_chunks):
        moments.append(moment_step(xs, ss, m, c, first_chunks))
    others = [lax.ppermute(a, "replica", twins) for a in moments]
    first_grad = scatter(partials_of(ss, w, n))
    outs, got, twin = [], [], []
    for c in range(first_chunks):
        *outs, mine = mean_step(place, moments[c], others[c], w, wp, c, outs)
        got.append(lax.ppermute(mine, "replica", partners))
    w, m = outs
    twin = [lax.ppermute(a, "replica", twins) for a in got]

    xs, ss = slopes_of(place, next_chains, w, out_grads[1])
    moments = []
    for c in range(last_chunks):
        moments.append(moment_step(xs, ss, m, c, last_chunks))
    others = [lax.ppermute(a, "replica", partners) for a in moments]
    last_grad = scatter(partials_of(ss, w, n))
    outs = []
    for c in range(last_chunks):
        outs = final_step(place, moments[c], others[c], w, got[c // 2], twin[c // 2], c, outs)
    return (outs[0][None], outs[1][None], jnp.stack([first_grad, last_grad]))


def solution(mesh):
    return jax.shard_map(
        local,
        mesh=mesh,
        in_specs=(
            P("replica", None, "tensor"),
            P("replica", None, "tensor"),
            P(None, ("replica", "tensor"), None),
            P(None, "replica", "tensor"),
        ),
        out_specs=(
            P("replica", None, "tensor"),
            P("replica", None, "tensor"),
            P(None, ("replica", "tensor"), None),
        ),
        check_vma=False,
    )
```
